512 devices in a mesh: band: 128 (over y, z, core), lon: 4 (over x).
Axes of the slice: x: 4, y: 8, z: 8, core: 2. Of those that a mesh axis runs over, the one named last changes fastest.
Arguments:
- state: bfloat16 [822, 256, 2048], P(None, 'band', 'lon'), may hold values from -6 to 6
- kernel: float32 [822, 3, 3], replicated, may hold values from -6 to 6
- w_state: bfloat16 [256, 822], replicated, may hold values from -0.21875 to 0.21875
- w_conv: bfloat16 [256, 822], replicated, may hold values from -0.21875 to 0.21875
- w_adj: bfloat16 [256, 822], replicated, may hold values from -0.875 to 0.875
- bias_in: float32 [256], replicated, may hold values from -6 to 6
- w_out: bfloat16 [822, 256], replicated, may hold values from -0.375 to 0.375
- obs_op: bfloat16 [96, 822], replicated, may hold values from -0.078125 to 0.078125
- observations: float32 [96, 128, 512], P(None, 'band', 'lon'), may hold values from -12 to 12
- obs_mask: int32 [96, 128, 512], P(None, 'band', 'lon'), may hold values 0 or 1
- dual_in: bfloat16 [96, 128, 512], P(None, 'band', 'lon'), may hold values from -6 to 6
- dual_res: bfloat16 [256, 96], replicated, may hold values from -0.625 to 0.625
- dual_prev: bfloat16 [256, 96], replicated, may hold values from -0.625 to 0.625
- dual_bias: float32 [256], replicated, may hold values from -6 to 6
- dual_out_w: bfloat16 [96, 256], replicated, may hold values from -0.375 to 0.375
- footprint: int32 [128, 4, 8, 4], P('band', 'lon'), may hold values from 0 to 127, all different within a row; in each aligned block of 8 rows (0 to 7, 8 to 15, ..., all dimensions but the last counted through in order) at most 2 rows name the same one
Outputs:
- state_out: bfloat16 [822, 256, 2048], P(None, 'band', 'lon')
- dual_out: bfloat16 [96, 128, 512], P(None, 'band', 'lon')
The draws below stay inside these ranges and needn't reach their ends.
Inputs may be any that keep to these rules, and one draw needn't show every extreme that they name: `footprint`: within the 8 column blocks of one pair (b, l), the 4 entries of a block differ, and no value appears more than 2 times; in some pairs one value appears exactly 2 times.
All inputs are finite; a program needn't handle non-finite values. No bound on the sum of `obs_mask` on one device may be relied on, other than what follows from the above.
Results may differ from the reference program's by a relative error of at most 0.0075.
Values may be sent and summed in bfloat16 or wider, within the bound.
No kernel may reach another device: no remote copies, remote signals or barrier semaphores. Data moves between devices by JAX's collectives and lax.ppermute only.
A program may use at most 64 MiB of HBM per device.

```python
import math
import jax
import jax.numpy as jnp
import numpy as np
from jax import lax

CH = 822
HID = 256
RADCH = 96
DHID = 256
PIX = 128
TOP = 4
LAT_DEV = 2
OWNERS = 128
NCBL = 4
CB_DEV = 8
MOST = 2
NLAT = 256
NLON = 2048
N_BAND = 128
N_LON = 4


def touch_ends(drawn, rng, smallest, top_value):
    extent = drawn.shape
    spot = [jax.random.randint(jax.random.fold_in(rng, axis), (), 0, extent[axis]) for axis in range(len(extent))]
    drawn = drawn.at[tuple(spot)].set(smallest)
    longest = extent.index(max(extent))
    spot[longest] = (spot[longest] + 1) % extent[longest]
    return drawn.at[tuple(spot)].set(top_value)


def block_scale(own_key, extent, split, low, top_value):
    level = 1.0
    for axis_at, blocks in split:
        heights = jax.random.uniform(jax.random.fold_in(jax.random.fold_in(own_key, 6), axis_at), (blocks,), jnp.float32, low / len(split), top_value / len(split))
        level = level * jnp.repeat(jnp.exp(heights), extent[axis_at] // blocks).reshape((-1,) + (1,) * (len(extent) - 1 - axis_at))
    return level


def routed_block(key, own, number, rows, count, top, reach, lean):
    sequence = jax.random.permutation(key, count)
    heavy_load, ordinary = portions_of(count, rows * top, reach, lean, True), portions_of(count, rows * top, reach, lean, False)
    places = jnp.arange(count)

    def named(tallies, offset_by):
        used = int((tallies > 0).sum())
        fixed = max(1, used // 4)
        passed = fixed + (places - fixed + offset_by * (used - fixed)) % max(1, count - fixed)
        return jnp.zeros((count,), jnp.int32).at[sequence[jnp.where(places < fixed, places, passed)]].set(jnp.asarray(tallies, jnp.int32))

    tallies = jnp.where(number % 4 == 0, named(heavy_load, number // 4), named(ordinary, number - number // 4 - 1))
    mixed = jax.random.permutation(jax.random.fold_in(own, 3), count)
    source_of, receiver = mixed[0:count // 2 * 2:2], mixed[1:count // 2 * 2:2]
    room = jnp.minimum(tallies[source_of] - 1, reach - tallies[receiver]) // 2
    room = jnp.where((source_of == sequence[0]) | (receiver == sequence[0]) | (tallies[receiver] == 0), 0, jnp.maximum(room, 0))
    passed = jax.random.randint(jax.random.fold_in(own, 4), (count // 2,), 0, 1 << 20) % (room + 1)
    tallies = tallies.at[source_of].add(-passed).at[receiver].add(passed)
    items = jnp.searchsorted(jnp.cumsum(tallies), jnp.arange(rows * top), side="right").astype(jnp.int32)
    table = items.reshape(top, rows).T
    table = table[jax.random.permutation(jax.random.fold_in(own, 1), rows)]
    offset_by = jax.random.randint(jax.random.fold_in(own, 2), (rows, 1), 0, top)
    return jnp.take_along_axis(table, (jnp.arange(top)[None, :] + offset_by) % top, axis=1)


def portions_of(number_of, total, most, lean, full):
    loads = [(1 << 20) // math.isqrt(standing ** lean) + 1 for standing in range(1, number_of + 1)]
    largest = most if full else min(most, max(-(-total // number_of), total * loads[0] // sum(loads)))
    least = 1 if total - largest >= number_of - 1 else 0
    counts, surplus = [largest] + [least] * (number_of - 1), total - largest - least * (number_of - 1)
    while surplus > 0:
        candidates = [i for i in range(1, number_of) if counts[i] < largest] or [i for i in range(1, number_of) if counts[i] < most]
        mass, remaining = sum([loads[i] for i in candidates]), surplus
        for i in candidates:
            more = min(most - counts[i], max(1, remaining * loads[i] // mass), surplus)
            counts[i] = counts[i] + more
            surplus = surplus - more
    return np.array(counts)


def noise(key, shape, scale, most, pieces=(), kind=jnp.bfloat16):
    values = jax.random.normal(key, shape, jnp.float32) * scale
    if len(pieces) > 0:
        values = block_scale(key, shape, pieces, -0.22, 0.18) * values
    return jnp.clip(values, min=-most, max=most).astype(kind)


def setup_inputs(seed: int = 0) -> dict:
    key_of = jax.random.split(jax.random.key(seed), 17)
    state = noise(key_of[0], (CH, NLAT, NLON), 1.0, 6.0, ((1, 128), (2, 4)))
    kernel = noise(key_of[1], (CH, 3, 3), 0.4, 6.0, (), jnp.float32)
    w_state = noise(key_of[2], (HID, CH), CH ** -0.5, 0.21875)
    w_conv = noise(key_of[3], (HID, CH), CH ** -0.5, 0.21875)
    w_adj = noise(key_of[4], (HID, CH), (CH // 16) ** -0.5, 0.875)
    bias_in = noise(key_of[5], (HID,), 1.0, 6.0, (), jnp.float32)
    w_out = noise(key_of[6], (CH, HID), HID ** -0.5, 0.375)
    obs_op = noise(key_of[7], (RADCH, CH), (CH * CB_DEV * TOP // 4) ** -0.5, 0.078125)
    observations = noise(key_of[8], (RADCH, OWNERS, NLON // NCBL), 2.0, 12.0, ((1, 128), (2, 4)), jnp.float32)
    obs_mask = touch_ends((jax.random.randint(key_of[9], (RADCH, OWNERS, NLON // NCBL), 0, 4) < 3).astype(jnp.int32), jax.random.fold_in(key_of[9], 1), 0, 1)
    dual_in = noise(key_of[10], (RADCH, OWNERS, NLON // NCBL), 1.0, 6.0, ((1, 128), (2, 4)))
    dual_res = noise(key_of[11], (DHID, RADCH), RADCH ** -0.5, 0.625)
    dual_prev = noise(key_of[12], (DHID, RADCH), RADCH ** -0.5, 0.625)
    dual_bias = noise(key_of[13], (DHID,), 1.0, 6.0, (), jnp.float32)
    dual_out_w = noise(key_of[14], (RADCH, DHID), DHID ** -0.5, 0.375)
    footprint_keys = jax.random.split(jax.random.fold_in(key_of[15], 1), N_BAND * N_LON * CB_DEV // CB_DEV)
    footprint_turns = jax.random.permutation(jax.random.fold_in(key_of[15], 3), N_BAND * N_LON * CB_DEV // CB_DEV)
    footprint = jax.vmap(lambda own, number: routed_block(jax.random.fold_in(key_of[15], 2), own, number, CB_DEV, OWNERS, TOP, MOST, 2))(footprint_keys, footprint_turns).reshape((N_BAND, N_LON, CB_DEV, TOP))
    return dict(state=state, kernel=kernel, w_state=w_state, w_conv=w_conv, w_adj=w_adj, bias_in=bias_in, w_out=w_out, obs_op=obs_op, observations=observations, obs_mask=obs_mask, dual_in=dual_in, dual_res=dual_res, dual_prev=dual_prev, dual_bias=dual_bias, dual_out_w=dual_out_w, footprint=footprint)


def reference(state, kernel, w_state, w_conv, w_adj, bias_in, w_out, obs_op, observations, obs_mask, dual_in, dual_res, dual_prev, dual_bias, dual_out_w, footprint):
    cover = jnp.sum((footprint[..., None] == jnp.arange(OWNERS, dtype=jnp.int32)).astype(jnp.float32), axis=3)
    operator32 = obs_op.astype(jnp.float32)
    bands = jnp.arange(N_BAND, dtype=jnp.int32)

    def forward(total, index):
        rows = lax.dynamic_slice_in_dim(state, (index * LAT_DEV).astype(jnp.int32), LAT_DEV, 1)
        cols = rows.reshape(CH, LAT_DEV, N_LON, NCBL, PIX).astype(jnp.float32)
        proj = jnp.einsum('rc,cilmp->limrp', operator32, cols).astype(jnp.bfloat16)
        proj = proj.reshape(N_LON, CB_DEV, RADCH, PIX).astype(jnp.float32)
        share = jnp.einsum('lkd,lkrp->rdlp', cover[index], proj).astype(jnp.bfloat16)
        share = lax.optimization_barrier(share)
        total = total + share.astype(jnp.float32)
        return total, None

    start = jnp.zeros((RADCH, OWNERS, N_LON, PIX), jnp.float32)
    evolved, unused = lax.scan(forward, start, bands)
    evolved = evolved.reshape(RADCH, OWNERS, N_LON * PIX)
    departure = jnp.where(obs_mask == 1, evolved - observations, 0.0).astype(jnp.bfloat16)
    pre = jnp.einsum('hr,rbn->hbn', dual_res.astype(jnp.float32), departure.astype(jnp.float32))
    pre = pre + jnp.einsum('hr,rbn->hbn', dual_prev.astype(jnp.float32), dual_in.astype(jnp.float32))
    dual_hidden = jax.nn.gelu(pre + dual_bias[:, None, None]).astype(jnp.bfloat16)
    dual_out = (dual_in.astype(jnp.float32) + jnp.einsum('rh,hbn->rbn', dual_out_w.astype(jnp.float32), dual_hidden.astype(jnp.float32))).astype(jnp.bfloat16)
    lam = dual_out.reshape(RADCH, OWNERS, N_LON, PIX).astype(jnp.float32)
    wrapped = jnp.concatenate([state[:, :, -1:], state, state[:, :, :1]], axis=2)
    padded = jnp.pad(wrapped, ((0, 0), (1, 1), (0, 0)))

    def primal(index):
        back = jnp.einsum('lkd,rdlp->lkrp', cover[index], lam).astype(jnp.bfloat16)
        adj = jnp.einsum('rc,lkrp->clkp', operator32, back.astype(jnp.float32)).astype(jnp.bfloat16)
        adj = adj.reshape(CH, N_LON, LAT_DEV, NCBL, PIX).transpose(0, 2, 1, 3, 4).reshape(CH, LAT_DEV * NLON)
        window = lax.dynamic_slice(padded, (jnp.int32(0), (index * LAT_DEV).astype(jnp.int32), jnp.int32(0)), (CH, LAT_DEV + 2, NLON + 2))
        conv = jnp.zeros((CH, LAT_DEV, NLON), jnp.float32)
        for a in range(3):
            for e in range(3):
                conv = conv + kernel[:, a, e][:, None, None] * window[:, a:a + LAT_DEV, e:e + NLON].astype(jnp.float32)
        conv = conv.astype(jnp.bfloat16).reshape(CH, LAT_DEV * NLON)
        rows = lax.dynamic_slice_in_dim(state, (index * LAT_DEV).astype(jnp.int32), LAT_DEV, 1).reshape(CH, LAT_DEV * NLON)
        pre_state = jnp.dot(w_state, rows, preferred_element_type=jnp.float32)
        pre_state = pre_state + jnp.dot(w_conv, conv, preferred_element_type=jnp.float32)
        pre_state = pre_state + jnp.dot(w_adj, adj, preferred_element_type=jnp.float32)
        hidden = jax.nn.gelu(pre_state + bias_in[:, None]).astype(jnp.bfloat16)
        result = rows.astype(jnp.float32) + jnp.dot(w_out, hidden, preferred_element_type=jnp.float32)
        return result.astype(jnp.bfloat16).reshape(CH, LAT_DEV, NLON)

    stacked = lax.map(primal, bands)
    state_out = stacked.transpose(1, 0, 2, 3).reshape(CH, NLAT, NLON)
    return state_out, dual_out
```

```python
import math

import jax
import jax.numpy as jnp
from jax import lax
from jax.experimental import pallas as pl
from jax.experimental.pallas import tpu as pltpu
from jax.sharding import PartitionSpec as P

PIX = 128
TOP = 4
SUB = 16

VMEM = pl.BlockSpec(memory_space=pltpu.MemorySpace.VMEM)
SMEM = pl.BlockSpec(memory_space=pltpu.MemorySpace.SMEM)


def across(a, b, dims):
    return lax.dot_general(a, b, (dims, ((), ())), preferred_element_type=jnp.float32)


def project_kernel(op_ref, flat_ref, z_ref):
    z = across(op_ref[...], flat_ref[...], ((1,), (0,))).astype(jnp.bfloat16)
    for k in range(z_ref.shape[0]):
        z_ref[k] = z[:, k * PIX : (k + 1) * PIX]


def scatter_kernel(slot_ref, own_ref, other_ref, out_ref):
    slots, blocks = (out_ref.shape[0], own_ref.shape[0])
    empty = jnp.zeros(out_ref.shape[1:], out_ref.dtype)

    def clear(i, carry):
        out_ref[i] = empty
        return carry

    lax.fori_loop(0, slots, clear, 0, unroll=4)
    for side, ref in enumerate((own_ref, other_ref)):
        for k in range(blocks):
            value = ref[k].astype(jnp.float32)
            for t in range(TOP):
                slot = slot_ref[(side * blocks + k) * TOP + t]

                @pl.when(slot < slots)
                def _(slot=slot, value=value):
                    total = out_ref[slot].astype(jnp.float32) + value
                    out_ref[slot] = total.astype(out_ref.dtype)


def gather_kernel(slot_ref, dual_ref, own_ref, other_ref):
    slots, blocks = (dual_ref.shape[0], own_ref.shape[0])
    for side, ref in enumerate((other_ref, own_ref)):
        side = 1 - side
        for k in range(blocks):
            total = jnp.zeros(dual_ref.shape[1:], jnp.float32)
            for t in range(TOP):
                slot = slot_ref[(side * blocks + k) * TOP + t]
                held = dual_ref[jnp.minimum(slot, slots - 1)].astype(jnp.float32)
                total = total + jnp.where(slot < slots, held, 0.0)
            ref[k] = total.astype(ref.dtype)


def stencil_kernel(
    flat_ref, taps_ref, edge_ref, ws_ref, wc_ref, local_ref, up_ref, down_ref, mixed_ref
):
    channels, columns = flat_ref.shape
    half = columns // 2
    column = lax.broadcasted_iota(jnp.int32, (SUB, half), 1)
    first, last = (column == 0, column == half - 1)

    def step(g, carry):
        rows = pl.ds(pl.multiple_of(g * SUB, SUB), SUB)
        taps = taps_ref[rows, :]
        edge = edge_ref[rows, :].astype(jnp.float32)

        def weight(a, e):
            n = a * 3 + e
            return taps[:, n : n + 1]

        views = []
        for i in range(2):
            x = flat_ref[rows, i * half : (i + 1) * half].astype(jnp.float32)
            left = jnp.where(first, edge[:, i : i + 1], pltpu.roll(x, 1, 1))
            right = jnp.where(last, edge[:, 2 + i : 3 + i], pltpu.roll(x, half - 1, 1))
            views.append((left, x, right))

        def row_sum(a, i):
            left, x, right = views[i]
            return weight(a, 0) * left + weight(a, 1) * x + weight(a, 2) * right

        parts = (
            row_sum(1, 0) + row_sum(2, 1),
            row_sum(0, 0) + row_sum(1, 1),
            row_sum(2, 0),
            row_sum(0, 1),
        )
        for n, part in enumerate(parts):
            mixed_ref[rows, n * half : (n + 1) * half] = part.astype(jnp.bfloat16)
        return carry

    lax.fori_loop(0, channels // SUB, step, 0)
    local_ref[...] = across(ws_ref[...], flat_ref[...], ((0,), (0,))) + across(
        wc_ref[...], mixed_ref[:, :columns], ((0,), (0,))
    )
    sent = across(wc_ref[...], mixed_ref[:, columns:], ((0,), (0,))).astype(jnp.bfloat16)
    up_ref[...] = sent[:, :half]
    down_ref[...] = sent[:, half:]


def update_kernel(
    local_ref, below_ref, above_ref, own_ref, other_ref, lift_ref, bias_ref, wo_ref, flat_ref,
    out_ref, back_ref,
):
    columns = flat_ref.shape[1]
    half = columns // 2
    for k in range(own_ref.shape[0]):
        back = own_ref[k] + other_ref[k].astype(jnp.float32)
        back_ref[:, k * PIX : (k + 1) * PIX] = back.astype(jnp.bfloat16)
    pre = local_ref[...] + across(lift_ref[...], back_ref[...], ((1,), (0,))) + bias_ref[...]
    edges = (above_ref, below_ref)
    for i in range(2):
        part = pre[:, i * half : (i + 1) * half] + edges[i][...].astype(jnp.float32)
        hidden = jax.nn.gelu(part).astype(jnp.bfloat16)
        update = across(wo_ref[...], hidden, ((1,), (0,)))
        before = flat_ref[:, i * half : (i + 1) * half].astype(jnp.float32)
        out_ref[:, i * half : (i + 1) * half] = (before + update).astype(out_ref.dtype)


def like(shape, dtype):
    return jax.ShapeDtypeStruct(shape, dtype)


def on_device(
    state,
    kernel,
    w_state,
    w_conv,
    w_adj,
    bias_in,
    w_out,
    obs_op,
    observations,
    obs_mask,
    dual_in,
    dual_res,
    dual_prev,
    dual_bias,
    dual_out_w,
    footprint,
):
    channels, lat_rows, lon_cols = state.shape
    radiance = obs_op.shape[0]
    hid = w_state.shape[0]
    owners = lax.axis_size("band")
    lon_count = lax.axis_size("lon")
    nblocks = lat_rows * lon_cols // PIX
    columns = lat_rows * lon_cols
    full = -(-channels // SUB) * SUB
    extra = full - channels
    side = math.isqrt(owners // 2)
    slots = side * side
    device = [[[(y * side + z) * 2 + c for c in range(2)] for z in range(side)] for y in range(side)]
    by_y = [[[device[y][z][c] for y in range(side)] for z in range(side)] for c in range(2)]
    by_z = [[[device[y][z][c] for z in range(side)] for y in range(side)] for c in range(2)]
    first, second = (by_y[0] + by_z[1], by_z[0] + by_y[1])
    swap = [(i, i ^ 1) for i in range(owners)]
    core = lax.axis_index("band") % 2

    def exchange(value, groups):
        return lax.all_to_all(
            value, "band", split_axis=0, concat_axis=0, axis_index_groups=groups, tiled=True
        )

    routes = footprint.reshape(nblocks * TOP)
    routes = jnp.concatenate([routes, lax.ppermute(routes, "band", swap)])
    at_y, at_z = (routes // (2 * side), (routes // 2) % side)
    slot = jnp.where(core == 0, at_y * side + at_z, at_z * side + at_y)
    slot = jnp.where(routes % 2 == core, slot, slots)

    flat = jnp.pad(state, ((0, extra), (0, 0), (0, 0))).reshape(full, columns)
    operator = jnp.pad(obs_op, ((0, 0), (0, extra)))
    projected = pl.pallas_call(
        project_kernel,
        out_shape=like((nblocks, radiance, PIX), jnp.bfloat16),
        in_specs=[VMEM, VMEM],
        out_specs=VMEM,
        name="project",
    )(operator, flat)
    projected_other = lax.ppermute(projected, "band", swap)
    shares = pl.pallas_call(
        scatter_kernel,
        out_shape=like((slots, radiance, PIX), jnp.bfloat16),
        in_specs=[SMEM, VMEM, VMEM],
        out_specs=VMEM,
        name="scatter",
    )(slot, projected, projected_other)
    arrived = exchange(shares, first)

    state_late, flat_late, projected_other = lax.optimization_barrier((state, flat, projected_other))
    up = [(i, (i + 1) % lon_count) for i in range(lon_count)]
    down = [(j, i) for i, j in up]
    before = lax.ppermute(state_late[:, :, lon_cols - 1].T, "lon", up)
    after = lax.ppermute(state_late[:, :, 0].T, "lon", down)
    edge = jnp.pad(jnp.concatenate([before, after], axis=0).T, ((0, extra), (0, 4)))
    taps = jnp.pad(kernel.reshape(channels, 9), ((0, extra), (0, 0)))
    local, to_up, to_down = pl.pallas_call(
        stencil_kernel,
        out_shape=(
            like((hid, columns), jnp.float32),
            like((hid, lon_cols), jnp.bfloat16),
            like((hid, lon_cols), jnp.bfloat16),
        ),
        in_specs=[VMEM] * 5,
        out_specs=(VMEM,) * 3,
        scratch_shapes=[pltpu.VMEM((full, 2 * columns), jnp.bfloat16)],
        name="stencil",
    )(
        flat_late,
        taps,
        edge,
        jnp.pad(w_state.T, ((0, extra), (0, 0))),
        jnp.pad(w_conv.T, ((0, extra), (0, 0))),
    )
    onward = [(i, i + 1) for i in range(owners - 1)]
    above = lax.ppermute(to_down, "band", onward)
    below = lax.ppermute(to_up, "band", [(j, i) for i, j in onward])
    lift = across(w_adj, obs_op, ((1,), (1,))).astype(jnp.bfloat16)

    summed = jnp.sum(
        arrived.reshape(side, side, radiance, PIX), axis=0, dtype=jnp.float32
    ).astype(jnp.bfloat16)
    evolved = jnp.sum(exchange(summed, second), axis=0, dtype=jnp.float32)

    observed = observations.reshape(radiance, PIX)
    valid = obs_mask.reshape(radiance, PIX)
    dual_now = dual_in.reshape(radiance, PIX)
    departure = jnp.where(valid == 1, evolved - observed, 0.0).astype(jnp.bfloat16)
    pre_dual = jnp.dot(dual_res, departure, preferred_element_type=jnp.float32)
    pre_dual = pre_dual + jnp.dot(dual_prev, dual_now, preferred_element_type=jnp.float32)
    dual_hidden = jax.nn.gelu(pre_dual + dual_bias[:, None]).astype(jnp.bfloat16)
    dual_new = (
        dual_now.astype(jnp.float32)
        + jnp.dot(dual_out_w, dual_hidden, preferred_element_type=jnp.float32)
    ).astype(jnp.bfloat16)

    column_of = exchange(jnp.broadcast_to(dual_new, (side, radiance, PIX)), second)
    all_of = exchange(
        jnp.broadcast_to(column_of, (side, side, radiance, PIX)).reshape(slots, radiance, PIX), first
    )
    back_own, back_other = pl.pallas_call(
        gather_kernel,
        out_shape=(
            like((nblocks, radiance, PIX), jnp.float32),
            like((nblocks, radiance, PIX), jnp.bfloat16),
        ),
        in_specs=[SMEM, VMEM],
        out_specs=(VMEM, VMEM),
        name="gather",
    )(slot, all_of)
    back_from = lax.ppermute(back_other, "band", swap)
    updated = pl.pallas_call(
        update_kernel,
        out_shape=like((full, columns), jnp.bfloat16),
        in_specs=[VMEM] * 9,
        out_specs=VMEM,
        scratch_shapes=[pltpu.VMEM((radiance, columns), jnp.bfloat16)],
        name="update",
    )(
        local,
        below,
        above,
        back_own,
        back_from,
        lift,
        bias_in[:, None],
        jnp.pad(w_out, ((0, extra), (0, 0))),
        flat,
    )
    state_out = updated.reshape(full, lat_rows, lon_cols)[:channels]
    return (state_out, dual_new.reshape(radiance, 1, PIX))


def solution(mesh):
    in_specs = (
        P(None, "band", "lon"),
        P(),
        P(),
        P(),
        P(),
        P(),
        P(),
        P(),
        P(None, "band", "lon"),
        P(None, "band", "lon"),
        P(None, "band", "lon"),
        P(),
        P(),
        P(),
        P(),
        P("band", "lon", None, None),
    )
    out_specs = (P(None, "band", "lon"), P(None, "band", "lon"))
    return jax.shard_map(
        on_device, mesh=mesh, in_specs=in_specs, out_specs=out_specs, check_vma=False
    )
```

```python
import math

import jax
import jax.numpy as jnp
from jax import lax
from jax.experimental import pallas as pl
from jax.experimental.pallas import tpu as pltpu
from jax.sharding import PartitionSpec as P

PIX = 128
TOP = 4
SUB = 16
CHUNK = 208

VMEM = pl.BlockSpec(memory_space=pltpu.MemorySpace.VMEM)
SMEM = pl.BlockSpec(memory_space=pltpu.MemorySpace.SMEM)


def across(a, b, dims):
    return lax.dot_general(a, b, (dims, ((), ())), preferred_element_type=jnp.float32)


def edges_kernel(first0_ref, first1_ref, last0_ref, last1_ref, first_ref, last_ref):
    lane = lax.broadcasted_iota(jnp.int32, first_ref.shape, 1)

    def pair(own, other, turn, at):
        turned = pltpu.roll(other[...].astype(jnp.float32), turn, 1)
        return jnp.where(lane == at, own[...].astype(jnp.float32), turned).astype(jnp.bfloat16)

    first_ref[...] = pair(first0_ref, first1_ref, 1, 0)
    last_ref[...] = pair(last0_ref, last1_ref, PIX - 1, PIX - 1)


def scatter_kernel(core_ref, own_route_ref, other_route_ref, own_ref, other_ref, out_ref, slot_ref):
    slots = out_ref.shape[0]
    side = math.isqrt(slots)
    blocks = own_ref.shape[1] // PIX
    core = core_ref[0]
    empty = jnp.zeros(out_ref.shape[1:], out_ref.dtype)

    def clear(i, carry):
        out_ref[i] = empty
        return carry

    lax.fori_loop(0, slots, clear, 0, unroll=8)
    for half, (route_ref, ref) in enumerate(((own_route_ref, own_ref), (other_route_ref, other_ref))):
        for k in range(blocks):
            value = ref[:, k * PIX : (k + 1) * PIX].astype(jnp.float32)
            for t in range(TOP):
                route = route_ref[k * TOP + t]
                at_y, at_z = (route // (2 * side), (route // 2) % side)
                slot = jnp.where(core == 0, at_y * side + at_z, at_z * side + at_y)
                slot = jnp.where(route % 2 == core, slot, slots)
                slot_ref[(half * blocks + k) * TOP + t] = slot

                @pl.when(slot < slots)
                def _(slot=slot, value=value):
                    total = out_ref[slot].astype(jnp.float32) + value
                    out_ref[slot] = total.astype(out_ref.dtype)


def gather_kernel(slot_ref, dual_ref, own_ref, other_ref):
    slots = dual_ref.shape[0]
    blocks = own_ref.shape[1] // PIX
    for half, ref in ((1, other_ref), (0, own_ref)):
        for k in range(blocks):
            total = jnp.zeros(dual_ref.shape[1:], jnp.float32)
            for t in range(TOP):
                slot = slot_ref[(half * blocks + k) * TOP + t]
                held = dual_ref[jnp.minimum(slot, slots - 1)].astype(jnp.float32)
                total = total + jnp.where(slot < slots, held, 0.0)
            ref[:, k * PIX : (k + 1) * PIX] = total.astype(ref.dtype)


def stencil_kernel(
    flat_ref, taps_ref, before_ref, after_ref, ws_ref, wc_ref, local_ref, up_ref, down_ref, mixed_ref
):
    full, columns = flat_ref.shape
    channels = ws_ref.shape[0]
    half = columns // 2
    column = lax.broadcasted_iota(jnp.int32, (SUB, half), 1)
    first, last = (column == 0, column == half - 1)

    def step(g, carry):
        rows = pl.ds(pl.multiple_of(g * SUB, SUB), SUB)
        taps = taps_ref[rows, :]
        before = before_ref[rows, :].astype(jnp.float32)
        after = after_ref[rows, :].astype(jnp.float32)

        def weight(a, e):
            n = a * 3 + e
            return taps[:, n : n + 1]

        views = []
        for i in range(2):
            x = flat_ref[rows, i * half : (i + 1) * half].astype(jnp.float32)
            left = jnp.where(first, before[:, PIX - 1 - i : PIX - i], pltpu.roll(x, 1, 1))
            right = jnp.where(last, after[:, i : i + 1], pltpu.roll(x, half - 1, 1))
            views.append((left, x, right))

        def row_sum(a, i):
            left, x, right = views[i]
            return weight(a, 0) * left + weight(a, 1) * x + weight(a, 2) * right

        parts = (
            row_sum(1, 0) + row_sum(2, 1),
            row_sum(0, 0) + row_sum(1, 1),
            row_sum(2, 0),
            row_sum(0, 1),
        )
        for n, part in enumerate(parts):
            mixed_ref[rows, n * half : (n + 1) * half] = part.astype(jnp.bfloat16)
        return carry

    lax.fori_loop(0, full // SUB, step, 0)
    local_ref[...] = across(ws_ref[...], flat_ref[:channels, :], ((0,), (0,))) + across(
        wc_ref[...], mixed_ref[:channels, :columns], ((0,), (0,))
    )
    sent = across(wc_ref[...], mixed_ref[:channels, columns:], ((0,), (0,))).astype(jnp.bfloat16)
    up_ref[...] = sent[:, :half]
    down_ref[...] = sent[:, half:]


def update_kernel(base_ref, own_ref, other_ref, lift_ref, wo_ref, flat_ref, out_ref, hidden_ref):
    half = flat_ref.shape[1] // 2

    @pl.when(pl.program_id(0) == 0)
    def _():
        back = (own_ref[...] + other_ref[...].astype(jnp.float32)).astype(jnp.bfloat16)
        pre = base_ref[...] + across(lift_ref[...], back, ((1,), (0,)))
        hidden_ref[...] = jax.nn.gelu(pre).astype(jnp.bfloat16)

    after = across(wo_ref[...], hidden_ref[...], ((1,), (0,))) + flat_ref[...].astype(jnp.float32)
    after = after.astype(out_ref.dtype)
    for i in range(2):
        out_ref[:, i, :] = after[:, i * half : (i + 1) * half]


def like(shape, dtype):
    return jax.ShapeDtypeStruct(shape, dtype)


def on_device(
    state,
    kernel,
    w_state,
    w_conv,
    w_adj,
    bias_in,
    w_out,
    obs_op,
    observations,
    obs_mask,
    dual_in,
    dual_res,
    dual_prev,
    dual_bias,
    dual_out_w,
    footprint,
):
    channels, lat_rows, lon_cols = state.shape
    radiance = obs_op.shape[0]
    hid = w_state.shape[0]
    owners = lax.axis_size("band")
    lon_count = lax.axis_size("lon")
    nblocks = lat_rows * lon_cols // PIX
    columns = lat_rows * lon_cols
    full = -(-channels // SUB) * SUB
    extra = full - channels
    side = math.isqrt(owners // 2)
    slots = side * side
    device = [[[(y * side + z) * 2 + c for c in range(2)] for z in range(side)] for y in range(side)]
    by_y = [[[device[y][z][c] for y in range(side)] for z in range(side)] for c in range(2)]
    by_z = [[[device[y][z][c] for z in range(side)] for y in range(side)] for c in range(2)]
    first, second = (by_y[0] + by_z[1], by_z[0] + by_y[1])
    swap = [(i, i ^ 1) for i in range(owners)]
    core = lax.axis_index("band") % 2

    def exchange(value, groups):
        return lax.all_to_all(
            value, "band", split_axis=0, concat_axis=0, axis_index_groups=groups, tiled=True
        )

    routes = footprint.reshape(nblocks * TOP)
    routes_other = lax.ppermute(routes, "band", swap)

    flat = jnp.pad(state, ((0, extra), (0, 0), (0, 0))).reshape(full, columns)
    projected = jnp.dot(
        obs_op, flat[:channels], preferred_element_type=jnp.float32
    ).astype(jnp.bfloat16)
    projected_other = lax.ppermute(projected, "band", swap)
    shares, slot = pl.pallas_call(
        scatter_kernel,
        out_shape=(
            like((slots, radiance, PIX), jnp.bfloat16),
            like((2 * nblocks * TOP,), jnp.int32),
        ),
        in_specs=[SMEM, SMEM, SMEM, VMEM, VMEM],
        out_specs=(VMEM, SMEM),
        name="scatter",
    )(core.reshape(1), routes, routes_other, projected, projected_other)
    arrived = exchange(shares, first)

    flat_late, _ = lax.optimization_barrier((flat, slot))
    up = [(i, (i + 1) % lon_count) for i in range(lon_count)]
    down = [(j, i) for i, j in up]
    lanes = [0, lon_cols // PIX, lon_cols // PIX - 1, columns // PIX - 1]
    initial, final = pl.pallas_call(
        edges_kernel,
        out_shape=(like((full, PIX), jnp.bfloat16),) * 2,
        grid=(1,),
        in_specs=[pl.BlockSpec((full, PIX), lambda i, n=n: (0, n)) for n in lanes],
        out_specs=(pl.BlockSpec((full, PIX), lambda i: (0, 0)),) * 2,
        name="edges",
    )(flat_late, flat_late, flat_late, flat_late)
    before = lax.ppermute(final, "lon", up)
    after = lax.ppermute(initial, "lon", down)
    taps = jnp.pad(kernel.reshape(channels, 9), ((0, extra), (0, 0)))
    local, to_up, to_down = pl.pallas_call(
        stencil_kernel,
        out_shape=(
            like((hid, columns), jnp.float32),
            like((hid, lon_cols), jnp.bfloat16),
            like((hid, lon_cols), jnp.bfloat16),
        ),
        in_specs=[VMEM] * 6,
        out_specs=(VMEM,) * 3,
        scratch_shapes=[pltpu.VMEM((full, 2 * columns), jnp.bfloat16)],
        name="stencil",
    )(flat_late, taps, before, after, w_state.T, w_conv.T)
    lift = across(w_adj, obs_op, ((1,), (1,))).astype(jnp.bfloat16)
    arrived, local, to_up, to_down, lift = lax.optimization_barrier(
        (arrived, local, to_up, to_down, lift)
    )

    summed = jnp.sum(
        arrived.reshape(side, side, radiance, PIX), axis=0, dtype=jnp.float32
    ).astype(jnp.bfloat16)
    evolved = jnp.sum(exchange(summed, second), axis=0, dtype=jnp.float32)

    observed = observations.reshape(radiance, PIX)
    valid = obs_mask.reshape(radiance, PIX)
    dual_now = dual_in.reshape(radiance, PIX)
    departure = jnp.where(valid == 1, evolved - observed, 0.0).astype(jnp.bfloat16)
    pre_dual = jnp.dot(dual_res, departure, preferred_element_type=jnp.float32)
    pre_dual = pre_dual + jnp.dot(dual_prev, dual_now, preferred_element_type=jnp.float32)
    dual_hidden = jax.nn.gelu(pre_dual + dual_bias[:, None]).astype(jnp.bfloat16)
    dual_new = (
        dual_now.astype(jnp.float32)
        + jnp.dot(dual_out_w, dual_hidden, preferred_element_type=jnp.float32)
    ).astype(jnp.bfloat16)

    column_of = exchange(jnp.broadcast_to(dual_new, (side, radiance, PIX)), second)
    spread = jnp.broadcast_to(column_of, (side, side, radiance, PIX)).reshape(slots, radiance, PIX)
    spread, to_up, to_down = lax.optimization_barrier((spread, to_up, to_down))
    all_of = exchange(spread, first)
    onward = [(i, i + 1) for i in range(owners - 1)]
    above = lax.ppermute(to_down, "band", onward)
    below = lax.ppermute(to_up, "band", [(j, i) for i, j in onward])
    base = local + jnp.concatenate([above, below], axis=1).astype(jnp.float32) + bias_in[:, None]
    all_of, base = lax.optimization_barrier((all_of, base))
    back_own, back_other = pl.pallas_call(
        gather_kernel,
        out_shape=(
            like((radiance, columns), jnp.float32),
            like((radiance, columns), jnp.bfloat16),
        ),
        in_specs=[SMEM, VMEM],
        out_specs=(VMEM, VMEM),
        name="gather",
    )(slot, all_of)
    back_from = lax.ppermute(back_other, "band", swap)

    def whole(*shape):
        return pl.BlockSpec(shape, lambda i: (0, 0))

    state_out = pl.pallas_call(
        update_kernel,
        out_shape=like(state.shape, jnp.bfloat16),
        grid=(-(-channels // CHUNK),),
        in_specs=[
            whole(hid, columns),
            whole(radiance, columns),
            whole(radiance, columns),
            whole(hid, radiance),
            pl.BlockSpec((CHUNK, hid), lambda i: (i, 0)),
            pl.BlockSpec((CHUNK, columns), lambda i: (i, 0)),
        ],
        out_specs=pl.BlockSpec((CHUNK, lat_rows, lon_cols), lambda i: (i, 0, 0)),
        scratch_shapes=[pltpu.VMEM((hid, columns), jnp.bfloat16)],
        name="update",
    )(base, back_own, back_from, lift, w_out, flat)
    return (state_out, dual_new.reshape(radiance, 1, PIX))


def solution(mesh):
    in_specs = (
        P(None, "band", "lon"),
        P(),
        P(),
        P(),
        P(),
        P(),
        P(),
        P(),
        P(None, "band", "lon"),
        P(None, "band", "lon"),
        P(None, "band", "lon"),
        P(),
        P(),
        P(),
        P(),
        P("band", "lon", None, None),
    )
    out_specs = (P(None, "band", "lon"), P(None, "band", "lon"))
    return jax.shard_map(
        on_device, mesh=mesh, in_specs=in_specs, out_specs=out_specs, check_vma=False
    )
```

```python
import math

import jax
import jax.numpy as jnp
from jax import lax
from jax.experimental import pallas as pl
from jax.experimental.pallas import tpu as pltpu
from jax.sharding import PartitionSpec as P

PIX = 128
TOP = 4
SUB = 16
CHUNK = 144

VMEM = pl.BlockSpec(memory_space=pltpu.MemorySpace.VMEM)
HBM = pl.BlockSpec(memory_space=pltpu.MemorySpace.HBM)
SMEM = pl.BlockSpec(memory_space=pltpu.MemorySpace.SMEM)


def across(a, b, dims):
    return lax.dot_general(a, b, (dims, ((), ())), preferred_element_type=jnp.float32)


def edges_kernel(first0_ref, first1_ref, last0_ref, last1_ref, first_ref, last_ref):
    lane = lax.broadcasted_iota(jnp.int32, first_ref.shape, 1)

    def pair(own, other, turn, at):
        turned = pltpu.roll(other[...].astype(jnp.float32), turn, 1)
        return jnp.where(lane == at, own[...].astype(jnp.float32), turned).astype(jnp.bfloat16)

    first_ref[...] = pair(first0_ref, first1_ref, 1, 0)
    last_ref[...] = pair(last0_ref, last1_ref, PIX - 1, PIX - 1)


def scatter_kernel(
    core_ref, own_route_ref, own_ref, other_ref, out_ref, slot_ref, wide_ref, route_ref, sem
):
    slots = out_ref.shape[0]
    side = math.isqrt(slots)
    bits = side.bit_length() - 1
    blocks = own_ref.shape[1] // PIX
    radiance = out_ref.shape[1]
    core = core_ref[0]
    empty = jnp.zeros(out_ref.shape[1:], out_ref.dtype)
    wide_ref[...] = other_ref[radiance:, :PIX].astype(jnp.float32).astype(jnp.int32)
    copy = pltpu.make_async_copy(wide_ref, route_ref, sem)
    copy.start()

    def clear(i, carry):
        out_ref[i] = empty
        return carry

    lax.fori_loop(0, slots, clear, 0, unroll=8)

    def place(half, ref, k):
        value = ref[:radiance, k * PIX : (k + 1) * PIX].astype(jnp.float32)
        for t in range(TOP):
            n = k * TOP + t
            route = own_route_ref[n] if half == 0 else route_ref[0, n]
            at = lax.shift_right_logical(route, 1)
            turned = (at & (side - 1)) * side + lax.shift_right_logical(at, bits)
            slot = jnp.where(core == 0, at, turned)
            slot = jnp.where((route & 1) == core, slot, slots)
            slot_ref[half * blocks * TOP + n] = slot

            @pl.when(slot < slots)
            def _(slot=slot, value=value):
                total = out_ref[slot].astype(jnp.float32) + value
                out_ref[slot] = total.astype(out_ref.dtype)

    for k in range(blocks):
        place(0, own_ref, k)
    copy.wait()
    for k in range(blocks):
        place(1, other_ref, k)


def gather_kernel(slot_ref, dual_ref, own_ref, other_ref):
    slots = dual_ref.shape[0]
    blocks = own_ref.shape[1] // PIX
    for half, ref in ((1, other_ref), (0, own_ref)):
        for k in range(blocks):
            total = jnp.zeros(dual_ref.shape[1:], jnp.float32)
            for t in range(TOP):
                slot = slot_ref[(half * blocks + k) * TOP + t]
                held = dual_ref[jnp.minimum(slot, slots - 1)].astype(jnp.float32)
                total = total + jnp.where(slot < slots, held, 0.0)
            ref[:, k * PIX : (k + 1) * PIX] = total.astype(ref.dtype)


def sum_kernel(far_ref, out_ref, part_ref, total_ref, sems):
    count = far_ref.shape[0]
    copies = [pltpu.make_async_copy(far_ref.at[i], part_ref.at[i], sems.at[i]) for i in range(count)]
    for copy in copies:
        copy.start()
    for i in range(0, count, 2):
        copies[i].wait()
        copies[i + 1].wait()
        for j in range(out_ref.shape[0]):
            pair = part_ref[i, j].astype(jnp.float32) + part_ref[i + 1, j].astype(jnp.float32)
            if i > 0:
                pair = total_ref[j] + pair
            if i + 2 < count:
                total_ref[j] = pair
            else:
                out_ref[j] = pair.astype(out_ref.dtype)


def stencil_kernel(
    flat_ref, taps_ref, before_ref, after_ref, wc_ref, local_ref, up_ref, down_ref, mixed_ref
):
    channels, columns = flat_ref.shape
    half = columns // 2

    def piece(rows, count):
        column = lax.broadcasted_iota(jnp.int32, (count, half), 1)
        first, last = (column == 0, column == half - 1)
        taps = taps_ref[rows, :]
        before = before_ref[rows, :].astype(jnp.float32)
        after = after_ref[rows, :].astype(jnp.float32)

        def weight(a, e):
            n = a * 3 + e
            return taps[:, n : n + 1]

        views = []
        for i in range(2):
            x = flat_ref[rows, i * half : (i + 1) * half].astype(jnp.float32)
            left = jnp.where(first, before[:, PIX - 1 - i : PIX - i], pltpu.roll(x, 1, 1))
            right = jnp.where(last, after[:, i : i + 1], pltpu.roll(x, half - 1, 1))
            views.append((left, x, right))

        def row_sum(a, i):
            left, x, right = views[i]
            return weight(a, 0) * left + weight(a, 1) * x + weight(a, 2) * right

        parts = (
            row_sum(1, 0) + row_sum(2, 1),
            row_sum(0, 0) + row_sum(1, 1),
            row_sum(2, 0),
            row_sum(0, 1),
        )
        for n, part in enumerate(parts):
            mixed_ref[rows, n * half : (n + 1) * half] = part.astype(jnp.bfloat16)

    steps = channels // SUB

    def step(g, carry):
        piece(pl.ds(pl.multiple_of(g * SUB, SUB), SUB), SUB)
        return carry

    lax.fori_loop(0, steps, step, 0, unroll=3)
    if channels > steps * SUB:
        piece(slice(steps * SUB, channels), channels - steps * SUB)
    sent = across(wc_ref[...], mixed_ref[:, columns:], ((0,), (0,))).astype(jnp.bfloat16)
    up_ref[...] = sent[:, :half]
    down_ref[...] = sent[:, half:]
    local_ref[...] = across(wc_ref[...], mixed_ref[:, :columns], ((0,), (0,)))


def update_kernel(
    base_ref, own_ref, other_ref, lift_ref, wo_ref, flat_ref, far_ref, hidden_ref, out_ref, sems
):
    channels, columns = flat_ref.shape
    half = columns // 2
    back = (own_ref[...] + other_ref[...].astype(jnp.float32)).astype(jnp.bfloat16)
    pre = base_ref[...] + across(lift_ref[...], back, ((1,), (0,)))
    hidden_ref[...] = jax.nn.gelu(pre).astype(jnp.bfloat16)
    copies = []
    for n, at in enumerate(range(0, channels, CHUNK)):
        rows = slice(at, min(at + CHUNK, channels))
        after = across(wo_ref[rows, :], hidden_ref[...], ((1,), (0,)))
        after = (after + flat_ref[rows, :].astype(jnp.float32)).astype(out_ref.dtype)
        for i in range(2):
            out_ref[rows, i, :] = after[:, i * half : (i + 1) * half]
        part = pl.ds(rows.start, rows.stop - rows.start)
        copy = pltpu.make_async_copy(out_ref.at[part], far_ref.at[part], sems.at[n])
        copy.start()
        copies.append(copy)
    for copy in copies:
        copy.wait()


def room(mebibytes):
    return pltpu.CompilerParams(vmem_limit_bytes=mebibytes * 1024 * 1024)


def like(shape, dtype):
    return jax.ShapeDtypeStruct(shape, dtype)


def on_device(
    state,
    kernel,
    w_state,
    w_conv,
    w_adj,
    bias_in,
    w_out,
    obs_op,
    observations,
    obs_mask,
    dual_in,
    dual_res,
    dual_prev,
    dual_bias,
    dual_out_w,
    footprint,
):
    channels, lat_rows, lon_cols = state.shape
    radiance = obs_op.shape[0]
    hid = w_state.shape[0]
    owners = lax.axis_size("band")
    lon_count = lax.axis_size("lon")
    nblocks = lat_rows * lon_cols // PIX
    columns = lat_rows * lon_cols
    side = math.isqrt(owners // 2)
    slots = side * side
    device = [[[(y * side + z) * 2 + c for c in range(2)] for z in range(side)] for y in range(side)]
    by_y = [[[device[y][z][c] for y in range(side)] for z in range(side)] for c in range(2)]
    by_z = [[[device[y][z][c] for z in range(side)] for y in range(side)] for c in range(2)]
    first, second = (by_y[0] + by_z[1], by_z[0] + by_y[1])
    swap = [(i, i ^ 1) for i in range(owners)]
    core = lax.axis_index("band") % 2

    def exchange(value, groups):
        return lax.all_to_all(
            value, "band", split_axis=0, concat_axis=0, axis_index_groups=groups, tiled=True
        )

    routes = footprint.reshape(nblocks * TOP)
    flat = state.reshape(channels, columns)
    projected = jnp.dot(obs_op, flat, preferred_element_type=jnp.float32).astype(jnp.bfloat16)
    rider = jnp.pad(routes.astype(jnp.bfloat16)[None], ((0, 7), (0, columns - nblocks * TOP)))
    projected = jnp.concatenate([projected, rider])
    projected_other = lax.ppermute(projected, "band", swap)
    shares, slot = pl.pallas_call(
        scatter_kernel,
        out_shape=(
            like((slots, radiance, PIX), jnp.bfloat16),
            like((2 * nblocks * TOP,), jnp.int32),
        ),
        in_specs=[SMEM, SMEM, VMEM, VMEM],
        out_specs=(VMEM, SMEM),
        scratch_shapes=[
            pltpu.VMEM((8, PIX), jnp.int32),
            pltpu.SMEM((8, PIX), jnp.int32),
            pltpu.SemaphoreType.DMA,
        ],
        compiler_params=room(8),
        name="scatter",
    )(core.reshape(1), routes, projected, projected_other)
    arrived = exchange(shares, first)

    flat_late, _ = lax.optimization_barrier((flat, slot))
    up = [(i, (i + 1) % lon_count) for i in range(lon_count)]
    down = [(j, i) for i, j in up]
    lanes = [0, lon_cols // PIX, lon_cols // PIX - 1, columns // PIX - 1]
    initial, final = pl.pallas_call(
        edges_kernel,
        out_shape=(like((channels, PIX), jnp.bfloat16),) * 2,
        grid=(1,),
        in_specs=[pl.BlockSpec((channels, PIX), lambda i, n=n: (0, n)) for n in lanes],
        out_specs=(pl.BlockSpec((channels, PIX), lambda i: (0, 0)),) * 2,
        compiler_params=room(4),
        name="edges",
    )(flat_late, flat_late, flat_late, flat_late)
    before = lax.ppermute(final, "lon", up)
    after = lax.ppermute(initial, "lon", down)
    taps = kernel.reshape(channels, 9)
    local, to_up, to_down = pl.pallas_call(
        stencil_kernel,
        out_shape=(
            like((hid, columns), jnp.float32),
            like((hid, lon_cols), jnp.bfloat16),
            like((hid, lon_cols), jnp.bfloat16),
        ),
        in_specs=[VMEM] * 5,
        out_specs=(VMEM,) * 3,
        scratch_shapes=[pltpu.VMEM((channels, 2 * columns), jnp.bfloat16)],
        compiler_params=room(20),
        name="stencil",
    )(flat_late, taps, before, after, w_conv.T)
    arrived, local, to_up, to_down = lax.optimization_barrier((arrived, local, to_up, to_down))

    summed = pl.pallas_call(
        sum_kernel,
        out_shape=like((side, radiance, PIX), jnp.bfloat16),
        in_specs=[HBM],
        out_specs=VMEM,
        scratch_shapes=[
            pltpu.VMEM((side, side, radiance, PIX), jnp.bfloat16),
            pltpu.VMEM((side, radiance, PIX), jnp.float32),
            pltpu.SemaphoreType.DMA((side,)),
        ],
        compiler_params=room(6),
        name="sum",
    )(arrived.reshape(side, side, radiance, PIX))
    summed, to_up, to_down = lax.optimization_barrier((summed, to_up, to_down))
    evolved = jnp.sum(exchange(summed, second), axis=0, dtype=jnp.float32)

    observed = observations.reshape(radiance, PIX)
    valid = obs_mask.reshape(radiance, PIX)
    dual_now = dual_in.reshape(radiance, PIX)
    departure = jnp.where(valid == 1, evolved - observed, 0.0).astype(jnp.bfloat16)
    pre_dual = jnp.dot(dual_res, departure, preferred_element_type=jnp.float32)
    pre_dual = pre_dual + jnp.dot(dual_prev, dual_now, preferred_element_type=jnp.float32)
    dual_hidden = jax.nn.gelu(pre_dual + dual_bias[:, None]).astype(jnp.bfloat16)
    dual_new = (
        dual_now.astype(jnp.float32)
        + jnp.dot(dual_out_w, dual_hidden, preferred_element_type=jnp.float32)
    ).astype(jnp.bfloat16)

    column_of = exchange(jnp.broadcast_to(dual_new, (side, radiance, PIX)), second)
    spread = jnp.broadcast_to(column_of, (side, side, radiance, PIX)).reshape(slots, radiance, PIX)
    spread, flat_last, obs_last = lax.optimization_barrier((spread, flat_late, obs_op))
    all_of = exchange(spread, first)
    onward = [(i, i + 1) for i in range(owners - 1)]
    above = lax.ppermute(to_down, "band", onward)
    below = lax.ppermute(to_up, "band", [(j, i) for i, j in onward])
    local = local + jnp.dot(w_state, flat_last, preferred_element_type=jnp.float32)
    base = local + jnp.concatenate([above, below], axis=1).astype(jnp.float32) + bias_in[:, None]
    lift = across(w_adj, obs_last, ((1,), (1,))).astype(jnp.bfloat16)
    all_of, base, lift = lax.optimization_barrier((all_of, base, lift))
    back_own, back_other = pl.pallas_call(
        gather_kernel,
        out_shape=(
            like((radiance, columns), jnp.float32),
            like((radiance, columns), jnp.bfloat16),
        ),
        in_specs=[SMEM, VMEM],
        out_specs=(VMEM, VMEM),
        compiler_params=room(8),
        name="gather",
    )(slot, all_of)
    back_from = lax.ppermute(back_other, "band", swap)

    state_out = pl.pallas_call(
        update_kernel,
        out_shape=like(state.shape, jnp.bfloat16),
        in_specs=[VMEM] * 6,
        out_specs=HBM,
        scratch_shapes=[
            pltpu.VMEM((hid, columns), jnp.bfloat16),
            pltpu.VMEM(state.shape, jnp.bfloat16),
            pltpu.SemaphoreType.DMA((-(-channels // CHUNK),)),
        ],
        compiler_params=room(16),
        name="update",
    )(base, back_own, back_from, lift, w_out, flat_last)
    return (state_out, dual_new.reshape(radiance, 1, PIX))


def solution(mesh):
    in_specs = (
        P(None, "band", "lon"),
        P(),
        P(),
        P(),
        P(),
        P(),
        P(),
        P(),
        P(None, "band", "lon"),
        P(None, "band", "lon"),
        P(None, "band", "lon"),
        P(),
        P(),
        P(),
        P(),
        P("band", "lon", None, None),
    )
    out_specs = (P(None, "band", "lon"), P(None, "band", "lon"))
    return jax.shard_map(
        on_device, mesh=mesh, in_specs=in_specs, out_specs=out_specs, check_vma=False
    )
```

```python
import math

import jax
import jax.numpy as jnp
from jax import lax
from jax.experimental import pallas as pl
from jax.experimental.pallas import tpu as pltpu
from jax.sharding import PartitionSpec as P

PIX = 128
TOP = 4
SUB = 16
CHUNK = 144

VMEM = pl.BlockSpec(memory_space=pltpu.MemorySpace.VMEM)
HBM = pl.BlockSpec(memory_space=pltpu.MemorySpace.HBM)
SMEM = pl.BlockSpec(memory_space=pltpu.MemorySpace.SMEM)


def across(a, b, dims):
    return lax.dot_general(a, b, (dims, ((), ())), preferred_element_type=jnp.float32)


def fetch_kernel(state_ref, out_ref, sem):
    rows = state_ref.shape[0]
    copy = pltpu.make_async_copy(state_ref, out_ref.at[pl.ds(0, rows)], sem)
    copy.start()
    spare = (out_ref.shape[0] - rows,) + tuple(out_ref.shape[1:])
    if spare[0] > 0:
        out_ref[rows:] = jnp.zeros(spare, out_ref.dtype)
    copy.wait()


def edges_kernel(first0_ref, first1_ref, last0_ref, last1_ref, first_ref, last_ref):
    lane = lax.broadcasted_iota(jnp.int32, first_ref.shape, 1)

    def pair(own, other, turn, at):
        turned = pltpu.roll(other[...].astype(jnp.float32), turn, 1)
        return jnp.where(lane == at, own[...].astype(jnp.float32), turned).astype(jnp.bfloat16)

    first_ref[...] = pair(first0_ref, first1_ref, 1, 0)
    last_ref[...] = pair(last0_ref, last1_ref, PIX - 1, PIX - 1)


def scatter_kernel(
    core_ref, own_route_ref, own_ref, other_ref, out_ref, slot_ref, wide_ref, route_ref, sem
):
    slots = out_ref.shape[0]
    side = math.isqrt(slots)
    bits = side.bit_length() - 1
    blocks = own_ref.shape[1] // PIX
    radiance = out_ref.shape[1]
    core = core_ref[0]
    empty = jnp.zeros(out_ref.shape[1:], out_ref.dtype)
    wide_ref[...] = other_ref[radiance:, :PIX].astype(jnp.float32).astype(jnp.int32)
    copy = pltpu.make_async_copy(wide_ref, route_ref, sem)
    copy.start()

    def clear(i, carry):
        out_ref[i] = empty
        return carry

    lax.fori_loop(0, slots, clear, 0, unroll=8)

    def place(half, ref, k):
        value = ref[:radiance, k * PIX : (k + 1) * PIX].astype(jnp.float32)
        for t in range(TOP):
            n = k * TOP + t
            route = own_route_ref[n] if half == 0 else route_ref[0, n]
            at = lax.shift_right_logical(route, 1)
            turned = (at & (side - 1)) * side + lax.shift_right_logical(at, bits)
            slot = jnp.where(core == 0, at, turned)
            slot = jnp.where((route & 1) == core, slot, slots)
            slot_ref[half * blocks * TOP + n] = slot

            @pl.when(slot < slots)
            def _(slot=slot, value=value):
                total = out_ref[slot].astype(jnp.float32) + value
                out_ref[slot] = total.astype(out_ref.dtype)

    for k in range(blocks):
        place(0, own_ref, k)
    copy.wait()
    for k in range(blocks):
        place(1, other_ref, k)


def gather_kernel(slot_ref, dual_ref, own_ref, other_ref):
    slots = dual_ref.shape[0]
    blocks = own_ref.shape[1] // PIX
    for half, ref in ((1, other_ref), (0, own_ref)):
        for k in range(blocks):
            total = jnp.zeros(dual_ref.shape[1:], jnp.float32)
            for t in range(TOP):
                slot = slot_ref[(half * blocks + k) * TOP + t]
                held = dual_ref[jnp.minimum(slot, slots - 1)].astype(jnp.float32)
                total = total + jnp.where(slot < slots, held, 0.0)
            ref[:, k * PIX : (k + 1) * PIX] = total.astype(ref.dtype)


def stencil_kernel(
    flat_ref, taps_ref, before_ref, after_ref, wc_ref, local_ref, up_ref, down_ref, mixed_ref
):
    channels, columns = (wc_ref.shape[0], flat_ref.shape[1])
    half = columns // 2

    def piece(rows, count):
        column = lax.broadcasted_iota(jnp.int32, (count, half), 1)
        first, last = (column == 0, column == half - 1)
        taps = taps_ref[rows, :]
        before = before_ref[rows, :].astype(jnp.float32)
        after = after_ref[rows, :].astype(jnp.float32)

        def weight(a, e):
            n = a * 3 + e
            return taps[:, n : n + 1]

        views = []
        for i in range(2):
            x = flat_ref[rows, i * half : (i + 1) * half].astype(jnp.float32)
            left = jnp.where(first, before[:, PIX - 1 - i : PIX - i], pltpu.roll(x, 1, 1))
            right = jnp.where(last, after[:, i : i + 1], pltpu.roll(x, half - 1, 1))
            views.append((left, x, right))

        def row_sum(a, i):
            left, x, right = views[i]
            return weight(a, 0) * left + weight(a, 1) * x + weight(a, 2) * right

        parts = (
            row_sum(1, 0) + row_sum(2, 1),
            row_sum(0, 0) + row_sum(1, 1),
            row_sum(2, 0),
            row_sum(0, 1),
        )
        for n, part in enumerate(parts):
            mixed_ref[rows, n * half : (n + 1) * half] = part.astype(jnp.bfloat16)

    steps = channels // SUB

    def step(g, carry):
        piece(pl.ds(pl.multiple_of(g * SUB, SUB), SUB), SUB)
        return carry

    lax.fori_loop(0, steps, step, 0, unroll=3)
    if channels > steps * SUB:
        piece(slice(steps * SUB, channels), channels - steps * SUB)
    sent = across(wc_ref[...], mixed_ref[:channels, columns:], ((0,), (0,))).astype(jnp.bfloat16)
    up_ref[...] = sent[:, :half]
    down_ref[...] = sent[:, half:]
    local_ref[...] = across(wc_ref[...], mixed_ref[:channels, :columns], ((0,), (0,)))


def update_kernel(
    base_ref, own_ref, other_ref, lift_ref, wo_ref, flat_ref, far_ref, hidden_ref, out_ref, sems
):
    channels, columns = (far_ref.shape[0], flat_ref.shape[1])
    half = columns // 2
    back = (own_ref[...] + other_ref[...].astype(jnp.float32)).astype(jnp.bfloat16)
    pre = base_ref[...] + across(lift_ref[...], back, ((1,), (0,)))
    hidden_ref[...] = jax.nn.gelu(pre).astype(jnp.bfloat16)
    copies = []
    for n, at in enumerate(range(0, channels, CHUNK)):
        rows = slice(at, min(at + CHUNK, channels))
        after = across(wo_ref[rows, :], hidden_ref[...], ((1,), (0,)))
        after = (after + flat_ref[rows, :].astype(jnp.float32)).astype(out_ref.dtype)
        for i in range(2):
            out_ref[rows, i, :] = after[:, i * half : (i + 1) * half]
        part = pl.ds(rows.start, rows.stop - rows.start)
        copy = pltpu.make_async_copy(out_ref.at[part], far_ref.at[part], sems.at[n])
        copy.start()
        copies.append(copy)
    for copy in copies:
        copy.wait()


def room(mebibytes):
    return pltpu.CompilerParams(vmem_limit_bytes=mebibytes * 1024 * 1024)


def like(shape, dtype):
    return jax.ShapeDtypeStruct(shape, dtype)


def on_device(
    state,
    kernel,
    w_state,
    w_conv,
    w_adj,
    bias_in,
    w_out,
    obs_op,
    observations,
    obs_mask,
    dual_in,
    dual_res,
    dual_prev,
    dual_bias,
    dual_out_w,
    footprint,
):
    channels, lat_rows, lon_cols = state.shape
    radiance = obs_op.shape[0]
    hid = w_state.shape[0]
    owners = lax.axis_size("band")
    lon_count = lax.axis_size("lon")
    nblocks = lat_rows * lon_cols // PIX
    columns = lat_rows * lon_cols
    side = math.isqrt(owners // 2)
    slots = side * side
    device = [[[(y * side + z) * 2 + c for c in range(2)] for z in range(side)] for y in range(side)]
    by_y = [[[device[y][z][c] for y in range(side)] for z in range(side)] for c in range(2)]
    by_z = [[[device[y][z][c] for z in range(side)] for y in range(side)] for c in range(2)]
    first, second = (by_y[0] + by_z[1], by_z[0] + by_y[1])
    swap = [(i, i ^ 1) for i in range(owners)]
    core = lax.axis_index("band") % 2

    def exchange(value, groups):
        return lax.all_to_all(
            value, "band", split_axis=0, concat_axis=0, axis_index_groups=groups, tiled=True
        )

    routes = footprint.reshape(nblocks * TOP)
    tall = -(-channels // 8) * 8
    flat = pl.pallas_call(
        fetch_kernel,
        out_shape=like((tall, lat_rows, lon_cols), jnp.bfloat16),
        in_specs=[HBM],
        out_specs=VMEM,
        scratch_shapes=[pltpu.SemaphoreType.DMA],
        compiler_params=room(4),
        name="fetch",
    )(state).reshape(tall, columns)
    flat = lax.optimization_barrier(flat)
    projected = jnp.dot(obs_op, flat[:channels], preferred_element_type=jnp.float32).astype(jnp.bfloat16)
    rider = jnp.pad(routes.astype(jnp.bfloat16)[None], ((0, 7), (0, columns - nblocks * TOP)))
    projected = jnp.concatenate([projected, rider])
    projected_other = lax.ppermute(projected, "band", swap)
    shares, slot = pl.pallas_call(
        scatter_kernel,
        out_shape=(
            like((slots, radiance, PIX), jnp.bfloat16),
            like((2 * nblocks * TOP,), jnp.int32),
        ),
        in_specs=[SMEM, SMEM, VMEM, VMEM],
        out_specs=(VMEM, SMEM),
        scratch_shapes=[
            pltpu.VMEM((8, PIX), jnp.int32),
            pltpu.SMEM((8, PIX), jnp.int32),
            pltpu.SemaphoreType.DMA,
        ],
        compiler_params=room(8),
        name="scatter",
    )(core.reshape(1), routes, projected, projected_other)
    arrived = exchange(shares, first)

    flat_late, _ = lax.optimization_barrier((flat, slot))
    up = [(i, (i + 1) % lon_count) for i in range(lon_count)]
    down = [(j, i) for i, j in up]
    lanes = [0, lon_cols // PIX, lon_cols // PIX - 1, columns // PIX - 1]
    initial, final = pl.pallas_call(
        edges_kernel,
        out_shape=(like((tall, PIX), jnp.bfloat16),) * 2,
        grid=(1,),
        in_specs=[pl.BlockSpec((tall, PIX), lambda i, n=n: (0, n)) for n in lanes],
        out_specs=(pl.BlockSpec((tall, PIX), lambda i: (0, 0)),) * 2,
        compiler_params=room(4),
        name="edges",
    )(flat_late, flat_late, flat_late, flat_late)
    before = lax.ppermute(final, "lon", up)
    after = lax.ppermute(initial, "lon", down)
    taps = kernel.reshape(channels, 9)
    local, to_up, to_down = pl.pallas_call(
        stencil_kernel,
        out_shape=(
            like((hid, columns), jnp.float32),
            like((hid, lon_cols), jnp.bfloat16),
            like((hid, lon_cols), jnp.bfloat16),
        ),
        in_specs=[VMEM] * 5,
        out_specs=(VMEM,) * 3,
        scratch_shapes=[pltpu.VMEM((-(-channels // SUB) * SUB, 2 * columns), jnp.bfloat16)],
        compiler_params=room(20),
        name="stencil",
    )(flat_late, taps, before, after, w_conv.T)
    lift = across(w_adj, obs_op, ((1,), (1,))).astype(jnp.bfloat16)
    arrived, local, to_up, to_down, lift = lax.optimization_barrier(
        (arrived, local, to_up, to_down, lift)
    )

    summed = jnp.sum(
        arrived.reshape(side, side, radiance, PIX), axis=0, dtype=jnp.float32
    ).astype(jnp.bfloat16)
    summed, to_up, to_down = lax.optimization_barrier((summed, to_up, to_down))
    evolved = jnp.sum(exchange(summed, second), axis=0, dtype=jnp.float32)

    observed = observations.reshape(radiance, PIX)
    valid = obs_mask.reshape(radiance, PIX)
    dual_now = dual_in.reshape(radiance, PIX)
    departure = jnp.where(valid == 1, evolved - observed, 0.0).astype(jnp.bfloat16)
    pre_dual = jnp.dot(dual_res, departure, preferred_element_type=jnp.float32)
    pre_dual = pre_dual + jnp.dot(dual_prev, dual_now, preferred_element_type=jnp.float32)
    dual_hidden = jax.nn.gelu(pre_dual + dual_bias[:, None]).astype(jnp.bfloat16)
    dual_new = (
        dual_now.astype(jnp.float32)
        + jnp.dot(dual_out_w, dual_hidden, preferred_element_type=jnp.float32)
    ).astype(jnp.bfloat16)

    column_of = exchange(jnp.broadcast_to(dual_new, (side, radiance, PIX)), second)
    spread = jnp.broadcast_to(column_of, (side, side, radiance, PIX)).reshape(slots, radiance, PIX)
    spread, flat_last = lax.optimization_barrier((spread, flat_late))
    all_of = exchange(spread, first)
    onward = [(i, i + 1) for i in range(owners - 1)]
    above = lax.ppermute(to_down, "band", onward)
    below = lax.ppermute(to_up, "band", [(j, i) for i, j in onward])
    local = local + jnp.dot(w_state, flat_last[:channels], preferred_element_type=jnp.float32)
    base = local + jnp.concatenate([above, below], axis=1).astype(jnp.float32) + bias_in[:, None]
    all_of, base = lax.optimization_barrier((all_of, base))
    back_own, back_other = pl.pallas_call(
        gather_kernel,
        out_shape=(
            like((radiance, columns), jnp.float32),
            like((radiance, columns), jnp.bfloat16),
        ),
        in_specs=[SMEM, VMEM],
        out_specs=(VMEM, VMEM),
        compiler_params=room(8),
        name="gather",
    )(slot, all_of)
    back_from = lax.ppermute(back_other, "band", swap)

    state_out = pl.pallas_call(
        update_kernel,
        out_shape=like(state.shape, jnp.bfloat16),
        in_specs=[VMEM] * 6,
        out_specs=HBM,
        scratch_shapes=[
            pltpu.VMEM((hid, columns), jnp.bfloat16),
            pltpu.VMEM(state.shape, jnp.bfloat16),
            pltpu.SemaphoreType.DMA((-(-channels // CHUNK),)),
        ],
        compiler_params=room(16),
        name="update",
    )(base, back_own, back_from, lift, w_out, flat_last)
    return (state_out, dual_new.reshape(radiance, 1, PIX))


def solution(mesh):
    in_specs = (
        P(None, "band", "lon"),
        P(),
        P(),
        P(),
        P(),
        P(),
        P(),
        P(),
        P(None, "band", "lon"),
        P(None, "band", "lon"),
        P(None, "band", "lon"),
        P(),
        P(),
        P(),
        P(),
        P("band", "lon", None, None),
    )
    out_specs = (P(None, "band", "lon"), P(None, "band", "lon"))
    return jax.shard_map(
        on_device, mesh=mesh, in_specs=in_specs, out_specs=out_specs, check_vma=False
    )
```
